256 devices in a mesh: lon: 32 (over y, z), lat: 8 (over x, core).
Axes of the slice: x: 4, y: 4, z: 8, core: 2. Of those that a mesh axis runs over, the one named last changes fastest.
Arguments:
- height: float32 [1024, 512, 1024], P(None, 'lon', 'lat'), may hold values from -1 to 1
- land_sea: int32 [512, 1024], P('lon', 'lat'), may hold values 0 or 1
- patterns: bfloat16 [512, 2, 512, 1024], P(None, None, 'lon', 'lat'), may hold values from -0.01171875 to 0.01171875
Outputs:
- covariance: float32 [32, 512, 512], P('lon', 'lat')
The draws below stay inside these ranges and needn't reach their ends.
All inputs are finite; a program needn't handle non-finite values. No bound on the sum of `land_sea` on one device may be relied on, other than what follows from the above.
Results may differ from the reference program's by a relative error of at most 0.0003.
The reference program's roundings to bfloat16 on the way count: a program that leaves them out, or rounds other values in their place, can miss the bound.
Values sent between devices are 32-bit elements; how exact they have to be, the bound alone decides.
A program may use at most 128 MiB of HBM per device.

```python
import math
import jax
import jax.numpy as jnp
from jax import lax

TIMES = 1024
K = 512
NLON = 512
NLAT = 1024
LAGS = 32


def draw_height(key, part):
    first, second = jax.random.split(key, 2)
    shape = (TIMES, NLON, NLAT)
    ramp = 1.0 + 2.0 * jnp.arange(NLON, dtype=jnp.float32) / max(NLON - 1, 1)
    rough = jax.random.uniform(second, shape, jnp.float32, 0.5, 1.5)
    noise = jax.random.truncated_normal(first, -4.0, 4.0, shape, jnp.float32)
    return 0.05 * ramp[:, None] * rough * noise


def set_ends(drawn, stream_key, smallest, largest):
    extent = drawn.shape
    index_at = [jax.random.randint(jax.random.fold_in(stream_key, axis), (), 0, extent[axis]) for axis in range(len(extent))]
    drawn = drawn.at[tuple(index_at)].set(smallest)
    longest = extent.index(max(extent))
    index_at[longest] = (index_at[longest] + 1) % extent[longest]
    return drawn.at[tuple(index_at)].set(largest)


def spiked(result, key, source, target, shards_of, factor):
    owner, partner = [(jnp.arange(result.shape[position]) // (result.shape[position] // shards_of)).reshape([-1 if axis == position else 1 for axis in range(result.ndim)]) for position in (source, target)]
    chosen = jax.random.permutation(key, shards_of)[partner]
    strong = (owner == chosen) | (owner == (partner + shards_of // 2) % shards_of)
    return jnp.where(strong, factor * result, result)


def level_of(key, shape, pieces, least, top_value):
    gain, own = 1.0, jax.random.fold_in(key, 6)
    for axis_at, shards_of in pieces:
        heights = jnp.exp(jax.random.uniform(jax.random.fold_in(own, axis_at), (shards_of,), jnp.float32, least / len(pieces), top_value / len(pieces)))
        gain = gain * jnp.repeat(heights, shape[axis_at] // shards_of).reshape([-1 if axis == axis_at else 1 for axis in range(len(shape))])
    return gain


def noise_with(own_key, shape, scale, reach, shards, heavy, held_as=jnp.bfloat16):
    array = scale * jax.random.normal(own_key, shape, jnp.float32)
    if shards:
        array = array * level_of(own_key, shape, shards, -0.22, 0.18)
    return jnp.clip(spiked(array, jax.random.fold_in(own_key, 3), *heavy), -reach, reach).astype(held_as)


def setup_inputs(seed: int = 0) -> dict:
    key_of = jax.random.split(jax.random.key(seed), 4)
    return {
        "height": draw_height(jax.random.fold_in(key_of[3], 71), 0),
        "land_sea": set_ends((jax.random.randint(key_of[1], (NLON, NLAT), 0, 5) < 4).astype(jnp.int32), jax.random.fold_in(key_of[1], 1), 0, 1),
        "patterns": noise_with(key_of[2], (K, 2, NLON, NLAT), (2 * NLON * NLAT) ** -0.5, 0.01171875, ((2, 32), (3, 8)), (2, 0, 32, 2.75)),
    }


GRAVITY = 9.81
ROTATION = 7.2921e-05
EARTH_RADIUS = 6371000.0
LAT_SOUTH = 20.0
LAT_SPAN = 45.0
LON_STEP = 1.0 / 12.0

def stencil_coefs(rows_index, total_rows):
    degrees = LAT_SOUTH + LAT_SPAN * (rows_index.astype(jnp.float32) + 0.5) / total_rows
    radians = degrees * (math.pi / 180.0)
    coriolis = 2.0 * ROTATION * jnp.sin(radians)
    north_step = EARTH_RADIUS * (LAT_SPAN / total_rows) * (math.pi / 180.0)
    east_step = EARTH_RADIUS * jnp.cos(radians) * (LON_STEP * math.pi / 180.0)
    return (-GRAVITY / (coriolis * 2.0 * north_step), GRAVITY / (coriolis * 2.0 * east_step))

def velocities(padded, coef_east, coef_north, ocean):
    lat_diff = padded[:, 1:-1, 2:] - padded[:, 1:-1, :-2]
    lon_diff = padded[:, 2:, 1:-1] - padded[:, :-2, 1:-1]
    return (coef_east * lat_diff * ocean, coef_north * lon_diff * ocean)

def reference(height, land_sea, patterns):
    ocean = land_sea.astype(jnp.float32)
    coef_east, coef_north = stencil_coefs(jnp.arange(NLAT, dtype=jnp.int32), NLAT)
    flat_patterns = patterns.reshape(K, 2 * NLON * NLAT)
    blocks = height.reshape(TIMES // 32, 32, NLON, NLAT)

    def one_block(days):
        padded = jnp.pad(days, ((0, 0), (1, 1), (1, 1)))
        east_vel, north_vel = velocities(padded, coef_east, coef_north, ocean)
        energy = jnp.sum(east_vel * east_vel + north_vel * north_vel)
        stacked = jnp.stack([east_vel, north_vel], axis=1).astype(jnp.bfloat16).reshape(32, 2 * NLON * NLAT)
        part = lax.dot_general(flat_patterns, stacked, (((1,), (1,)), ((), ())), preferred_element_type=jnp.float32)
        return (part, energy)
    parts, energies = lax.map(one_block, blocks)
    totals = jnp.transpose(parts, (1, 0, 2)).reshape(K, TIMES)
    energy = jnp.sum(energies)
    centered = totals - lax.optimization_barrier(jnp.mean(totals, axis=1, keepdims=True))
    normed = centered / jnp.sqrt(energy / (2.0 * TIMES * NLON * NLAT) + 1e-06)
    padded_modes = jnp.concatenate([normed, jnp.zeros_like(normed)], axis=1)

    def one_lag(lag):
        shifted = lax.dynamic_slice_in_dim(padded_modes, lag, TIMES, 1)
        product = lax.dot_general(shifted, normed, (((1,), (1,)), ((), ())), precision=lax.Precision.HIGHEST, preferred_element_type=jnp.float32)
        return product / (TIMES - lag).astype(jnp.float32)
    return lax.map(one_lag, jnp.arange(LAGS, dtype=jnp.int32))
```

```python
import math

from jax.sharding import PartitionSpec as P

import jax
import jax.numpy as jnp
from jax import lax
from jax.experimental import pallas as pl
from jax.experimental.pallas import tpu as pltpu

MESH = pl.DeviceIdType.MESH


def allreduce_kernel(tot, en, out, eout, rc, acc, r2, acc2, r3, acc3, r4, er, ea,
                     s_core, v_core, s_mid, v_mid, s_z, v_z, s_e, v_e):
    lon = lax.axis_index("lon")
    lat = lax.axis_index("lat")
    y, z = lon // 8, lon % 8
    x, c = lat // 2, lat % 2
    partner = (lon, x * 2 + (1 - c))

    def at_x(d):
        return (lon, ((x + d) % 4) * 2 + c)

    def at_y(d):
        return (((y + d) % 4) * 8 + z, lat)

    def at_z(d):
        return (y * 8 + (z + d) % 8, lat)

    pending = []

    def send(src, dst, ssem, rsem, dev):
        copy = pltpu.make_async_remote_copy(
            src_ref=src, dst_ref=dst, send_sem=ssem, recv_sem=rsem,
            device_id=dev, device_id_type=MESH)
        copy.start()
        pending.append(copy)
        return copy

    barrier = pltpu.get_barrier_semaphore()
    peers = [partner] + [at_x(d) for d in (1, 2, 3)] + [at_y(d) for d in (1, 2, 3)]
    peers += [at_z(d) for d in range(1, 8)]
    for dev in peers:
        pl.semaphore_signal(barrier, inc=1, device_id=dev, device_id_type=MESH)
    pl.semaphore_wait(barrier, len(peers))

    first = (x, y)
    second = (y, x)
    at_first = (at_x, at_y)
    at_second = (at_y, at_x)
    order = (2, 1, 3, 0)

    def rows_of(core, q):
        return pl.ds(pl.multiple_of(core * 256 + q * 64, 64), 64)

    lanes = (pl.ds(0, 512), pl.ds(512, 512))

    e0 = send(en, er.at[0], s_e.at[0], v_e.at[0], partner)
    core = {}
    for d in order:
        for h in (0, 1):
            q = (first[h] + d) % 4
            core[h, d] = send(tot.at[rows_of(1 - c, q), lanes[h]], rc.at[h, d],
                              s_core.at[h * 4 + d], v_core.at[h * 4 + d], partner)
    mid = {}
    for d in order:
        for h in (0, 1):
            q = (first[h] + d) % 4
            core[h, d].wait_recv()
            acc[h, d] = tot[rows_of(c, q), lanes[h]] + rc[h, d]
            if d:
                mid[h, d] = send(acc.at[h, d], r2.at[h, d - 1], s_mid.at[h * 3 + d - 1],
                                 v_mid.at[h * 3 + d - 1], at_first[h](d))
    e0.wait_recv()
    ea[0] = en[...] + er[0]
    ex = [send(ea.at[0], er.at[d], s_e.at[d], v_e.at[d], at_x(d)) for d in (1, 2, 3)]
    mid2 = {}
    for h in (0, 1):
        for d in (1, 3, 2):
            mid[h, d].wait_recv()
        acc2[h] = (acc[h, 0] + r2[h, 0]) + (r2[h, 1] + r2[h, 2])
        for d in (2, 1, 3):
            q = (second[h] + d) % 4
            mid2[h, d] = send(acc2.at[h, pl.ds(pl.multiple_of(q * 16, 16), 16)], r3.at[h, d - 1],
                              s_mid.at[6 + h * 3 + d - 1], v_mid.at[6 + h * 3 + d - 1],
                              at_second[h](d))
    for copy in ex:
        copy.wait_recv()
    ea[1] = (ea[0] + er[1]) + (er[2] + er[3])
    ey = [send(ea.at[1], er.at[3 + d], s_e.at[3 + d], v_e.at[3 + d], at_y(d)) for d in (1, 2, 3)]
    zorder = (4, 3, 5, 2, 6, 1, 7)
    zc = {}

    def zblock(zq):
        return pl.ds(pl.multiple_of((zq // 4) * 8, 8), 8), zq % 4

    for h in (0, 1):
        for d in (1, 3, 2):
            mid2[h, d].wait_recv()
        acc3[h] = (acc2[h, pl.ds(pl.multiple_of(second[h] * 16, 16), 16)] + r3[h, 0]) + (
            r3[h, 1] + r3[h, 2])
        for d in zorder:
            r, l = zblock((z + d) % 8)
            zc[h, d] = send(acc3.at[h, r, pl.ds(pl.multiple_of(l * 128, 128), 128)],
                            r4.at[h, d - 1], s_z.at[h * 7 + d - 1], v_z.at[h * 7 + d - 1], at_z(d))
    for copy in ey:
        copy.wait_recv()
    ea[2] = (ea[1] + er[4]) + (er[5] + er[6])
    ez = [send(ea.at[2], er.at[6 + d], s_e.at[6 + d], v_e.at[6 + d], at_z(d)) for d in range(1, 8)]

    base = [pl.multiple_of(c * 256 + first[h] * 64 + second[h] * 16, 16) for h in (0, 1)]
    gz = {}
    for h in (0, 1):
        for d in (1, 7, 2, 6, 3, 5, 4):
            zc[h, d].wait_recv()
        r, l = zblock(z)
        mine = acc3[h, r, pl.ds(pl.multiple_of(l * 128, 128), 128)]
        mine = ((mine + r4[h, 0]) + (r4[h, 1] + r4[h, 2])) + (
            (r4[h, 3] + r4[h, 4]) + (r4[h, 5] + r4[h, 6]))
        place = (pl.ds(pl.multiple_of(base[h] + (z // 4) * 8, 8), 8),
                 pl.ds(pl.multiple_of(h * 512 + l * 128, 128), 128))
        out[place] = mine
        for d in zorder:
            gz[h, d] = send(out.at[place], out.at[place], s_z.at[14 + h * 7 + d - 1],
                            v_z.at[14 + h * 7 + d - 1], at_z(d))
    for copy in ez:
        copy.wait_recv()
    total = ea[2]
    for d in range(1, 8):
        total = total + er[6 + d]
    eout[...] = total

    g2 = {}
    for h in (0, 1):
        for d in (1, 7, 2, 6, 3, 5, 4):
            gz[h, d].wait_recv()
        region = out.at[pl.ds(base[h], 16), lanes[h]]
        for d in (2, 1, 3):
            g2[h, d] = send(region, region, s_mid.at[12 + h * 3 + d - 1],
                            v_mid.at[12 + h * 3 + d - 1], at_second[h](d))
    g1 = {}
    gc = {}
    for h in (0, 1):
        for d in (1, 3, 2):
            g2[h, d].wait_recv()
        region = out.at[rows_of(c, first[h]), lanes[h]]
        for d in (2, 1, 3):
            g1[h, d] = send(region, region, s_mid.at[18 + h * 3 + d - 1],
                            v_mid.at[18 + h * 3 + d - 1], at_first[h](d))
        gc[h, 0] = send(region, region, s_core.at[8 + h * 4], v_core.at[8 + h * 4], partner)
    for d in (1, 3, 2):
        for h in (0, 1):
            g1[h, d].wait_recv()
            region = out.at[rows_of(c, (first[h] + 4 - d) % 4), lanes[h]]
            gc[h, d] = send(region, region, s_core.at[8 + h * 4 + d], v_core.at[8 + h * 4 + d],
                            partner)
    for d in (0, 1, 3, 2):
        for h in (0, 1):
            gc[h, d].wait_recv()
    for copy in pending:
        copy.wait_send()


def allreduce(tot, en, collective_id=0):
    f32 = jnp.float32
    vm = pl.BlockSpec(memory_space=pltpu.VMEM)
    return pl.pallas_call(
        allreduce_kernel,
        out_shape=[jax.ShapeDtypeStruct((512, 1024), f32), jax.ShapeDtypeStruct((8, 128), f32)],
        in_specs=[vm, vm],
        out_specs=[vm, vm],
        scratch_shapes=[
            pltpu.VMEM((2, 4, 64, 512), f32),
            pltpu.VMEM((2, 4, 64, 512), f32),
            pltpu.VMEM((2, 3, 64, 512), f32),
            pltpu.VMEM((2, 64, 512), f32),
            pltpu.VMEM((2, 3, 16, 512), f32),
            pltpu.VMEM((2, 16, 512), f32),
            pltpu.VMEM((2, 7, 8, 128), f32),
            pltpu.VMEM((14, 8, 128), f32),
            pltpu.VMEM((3, 8, 128), f32),
            pltpu.SemaphoreType.DMA((16,)), pltpu.SemaphoreType.DMA((16,)),
            pltpu.SemaphoreType.DMA((24,)), pltpu.SemaphoreType.DMA((24,)),
            pltpu.SemaphoreType.DMA((28,)), pltpu.SemaphoreType.DMA((28,)),
            pltpu.SemaphoreType.DMA((14,)), pltpu.SemaphoreType.DMA((14,)),
        ],
        compiler_params=pltpu.CompilerParams(collective_id=collective_id, has_side_effects=True),
    )(tot, en)


LAG_DEV = 1


GRAVITY = 9.81
ROTATION = 7.2921e-05
EARTH_RADIUS = 6371000.0
LAT_SOUTH = 20.0
LAT_SPAN = 45.0
LON_STEP = 1.0 / 12.0


def padded_2(shard, sides, width):
    for axis, dim in sides:
        devices, length = (lax.axis_size(axis), shard.shape[dim])
        up = [(i, (i + 1) % devices) for i in range(devices - 1)]
        down = [(j, i) for i, j in up]
        last = lax.slice_in_dim(shard, length - width, length, axis=dim)
        initial = lax.slice_in_dim(shard, 0, width, axis=dim)
        before = lax.ppermute(last, axis, up)
        after = lax.ppermute(initial, axis, down)
        shard = jnp.concatenate([before, shard, after], axis=dim)
    return shard


def stencil_coefs(rows_index, total_rows):
    degrees = LAT_SOUTH + LAT_SPAN * (rows_index.astype(jnp.float32) + 0.5) / total_rows
    radians = degrees * (math.pi / 180.0)
    coriolis = 2.0 * ROTATION * jnp.sin(radians)
    north_step = EARTH_RADIUS * (LAT_SPAN / total_rows) * (math.pi / 180.0)
    east_step = EARTH_RADIUS * jnp.cos(radians) * (LON_STEP * math.pi / 180.0)
    return (-GRAVITY / (coriolis * 2.0 * north_step), GRAVITY / (coriolis * 2.0 * east_step))


def velocities(padded, coef_east, coef_north, ocean):
    lat_diff = padded[:, 1:-1, 2:] - padded[:, 1:-1, :-2]
    lon_diff = padded[:, 2:, 1:-1] - padded[:, :-2, 1:-1]
    return (coef_east * lat_diff * ocean, coef_north * lon_diff * ocean)


def on_device(height, land_sea, patterns):
    days, lon_cells, lat_cells = height.shape
    lat_devices = lax.axis_size("lat")
    lon_devices = lax.axis_size("lon")
    total_rows = lat_cells * lat_devices
    lat_place = lax.axis_index("lat")
    lon_place = lax.axis_index("lon")
    rows_index = lat_place * lat_cells + jnp.arange(lat_cells, dtype=jnp.int32)
    coef_east, coef_north = stencil_coefs(rows_index, total_rows)
    ocean = land_sea.astype(jnp.float32)
    padded = padded_2(height, (("lon", 1), ("lat", 2)), 1)
    east_vel, north_vel = velocities(padded, coef_east, coef_north, ocean)
    local_energy = jnp.sum(east_vel * east_vel + north_vel * north_vel)
    stacked = (
        jnp.stack([east_vel, north_vel], axis=1)
        .astype(jnp.bfloat16)
        .reshape(days, 2 * lon_cells * lat_cells)
    )
    mode_count = patterns.shape[0]
    owned = mode_count // lat_devices
    flat_patterns = patterns.reshape(mode_count, 2 * lon_cells * lat_cells)
    part = lax.dot_general(
        flat_patterns, stacked, (((1,), (1,)), ((), ())), preferred_element_type=jnp.float32
    )
    totals, energies = allreduce(part, jnp.full((8, 128), local_energy * (1.0 / 1024.0)))
    energy = jnp.sum(energies)
    cell_total = 2.0 * days * lon_cells * lon_devices * total_rows
    centered = totals - jnp.mean(totals, axis=1, keepdims=True)
    normed = centered / jnp.sqrt(energy / cell_total + 1e-06)
    my_rows = lax.dynamic_slice_in_dim(normed, lat_place * owned, owned, 0)
    padded_rows = jnp.concatenate([my_rows, jnp.zeros_like(my_rows)], axis=1)
    lag = lon_place * LAG_DEV + 0
    shifted = lax.dynamic_slice_in_dim(padded_rows, lag, days, 1)
    product = lax.dot_general(
        shifted,
        normed,
        (((1,), (1,)), ((), ())),
        precision=lax.Precision.HIGHEST,
        preferred_element_type=jnp.float32,
    )
    results = [product / (days - lag).astype(jnp.float32)]
    return jnp.stack(results, axis=0)


def solution(mesh):
    placed = (P(None, "lon", "lat"), P("lon", "lat"), P(None, None, "lon", "lat"))
    return jax.shard_map(
        on_device, mesh=mesh, in_specs=placed, out_specs=P("lon", "lat", None), check_vma=False
    )
```

```python
import math

import jax
import jax.numpy as jnp
from jax import lax
from jax.experimental import pallas as pl
from jax.experimental.pallas import tpu as pltpu
from jax.sharding import PartitionSpec as P

LAG_DEV = 1


GRAVITY = 9.81
ROTATION = 7.2921e-05
EARTH_RADIUS = 6371000.0
LAT_SOUTH = 20.0
LAT_SPAN = 45.0
LON_STEP = 1.0 / 12.0

MESH = pl.DeviceIdType.MESH


def allreduce_kernel(tot, en, out, eout, rc, acc, r2, acc2, r3, acc3, r4, er, ea,
                     s_core, v_core, s_mid, v_mid, s_z, v_z, s_e, v_e):
    lon = lax.axis_index("lon")
    lat = lax.axis_index("lat")
    y, z = lon // 8, lon % 8
    x, c = lat // 2, lat % 2
    partner = (lon, x * 2 + (1 - c))

    def at_x(d):
        return (lon, ((x + d) % 4) * 2 + c)

    def at_y(d):
        return (((y + d) % 4) * 8 + z, lat)

    def at_z(d):
        return (y * 8 + (z + d) % 8, lat)

    pending = []

    def send(src, dst, ssem, rsem, dev):
        copy = pltpu.make_async_remote_copy(
            src_ref=src, dst_ref=dst, send_sem=ssem, recv_sem=rsem,
            device_id=dev, device_id_type=MESH)
        copy.start()
        pending.append(copy)
        return copy

    barrier = pltpu.get_barrier_semaphore()
    peers = [partner] + [at_x(d) for d in (1, 2, 3)] + [at_y(d) for d in (1, 2, 3)]
    peers += [at_z(d) for d in range(1, 8)]
    for dev in peers:
        pl.semaphore_signal(barrier, inc=1, device_id=dev, device_id_type=MESH)
    pl.semaphore_wait(barrier, len(peers))

    first = (x, y)
    second = (y, x)
    at_first = (at_x, at_y)
    at_second = (at_y, at_x)
    order = (2, 1, 3, 0)

    def rows_of(core, q):
        return pl.ds(pl.multiple_of(core * 256 + q * 64, 64), 64)

    lanes = (pl.ds(0, 512), pl.ds(512, 512))

    e0 = send(en, er.at[0], s_e.at[0], v_e.at[0], partner)
    core = {}
    for d in order:
        for h in (0, 1):
            q = (first[h] + d) % 4
            core[h, d] = send(tot.at[rows_of(1 - c, q), lanes[h]], rc.at[h, d],
                              s_core.at[h * 4 + d], v_core.at[h * 4 + d], partner)
    mid = {}
    for d in order:
        for h in (0, 1):
            q = (first[h] + d) % 4
            core[h, d].wait_recv()
            acc[h, d] = tot[rows_of(c, q), lanes[h]] + rc[h, d]
            if d:
                mid[h, d] = send(acc.at[h, d], r2.at[h, d - 1], s_mid.at[h * 3 + d - 1],
                                 v_mid.at[h * 3 + d - 1], at_first[h](d))
    e0.wait_recv()
    ea[0] = en[...] + er[0]
    ex = [send(ea.at[0], er.at[d], s_e.at[d], v_e.at[d], at_x(d)) for d in (1, 2, 3)]
    mid2 = {}
    for h in (0, 1):
        for d in (1, 3, 2):
            mid[h, d].wait_recv()
        acc2[h] = (acc[h, 0] + r2[h, 0]) + (r2[h, 1] + r2[h, 2])
        for d in (2, 1, 3):
            q = (second[h] + d) % 4
            mid2[h, d] = send(acc2.at[h, pl.ds(pl.multiple_of(q * 16, 16), 16)], r3.at[h, d - 1],
                              s_mid.at[6 + h * 3 + d - 1], v_mid.at[6 + h * 3 + d - 1],
                              at_second[h](d))
    for copy in ex:
        copy.wait_recv()
    ea[1] = (ea[0] + er[1]) + (er[2] + er[3])
    ey = [send(ea.at[1], er.at[3 + d], s_e.at[3 + d], v_e.at[3 + d], at_y(d)) for d in (1, 2, 3)]
    zorder = (4, 3, 5, 2, 6, 1, 7)
    zc = {}

    def zblock(zq):
        return pl.ds(pl.multiple_of((zq // 4) * 8, 8), 8), zq % 4

    for h in (0, 1):
        for d in (1, 3, 2):
            mid2[h, d].wait_recv()
        acc3[h] = (acc2[h, pl.ds(pl.multiple_of(second[h] * 16, 16), 16)] + r3[h, 0]) + (
            r3[h, 1] + r3[h, 2])
        for d in zorder:
            r, l = zblock((z + d) % 8)
            zc[h, d] = send(acc3.at[h, r, pl.ds(pl.multiple_of(l * 128, 128), 128)],
                            r4.at[h, d - 1], s_z.at[h * 7 + d - 1], v_z.at[h * 7 + d - 1], at_z(d))
    for copy in ey:
        copy.wait_recv()
    ea[2] = (ea[1] + er[4]) + (er[5] + er[6])
    ez = [send(ea.at[2], er.at[6 + d], s_e.at[6 + d], v_e.at[6 + d], at_z(d)) for d in range(1, 8)]

    base = [pl.multiple_of(c * 256 + first[h] * 64 + second[h] * 16, 16) for h in (0, 1)]
    gz = {}
    for h in (0, 1):
        for d in (1, 7, 2, 6, 3, 5, 4):
            zc[h, d].wait_recv()
        r, l = zblock(z)
        mine = acc3[h, r, pl.ds(pl.multiple_of(l * 128, 128), 128)]
        mine = ((mine + r4[h, 0]) + (r4[h, 1] + r4[h, 2])) + (
            (r4[h, 3] + r4[h, 4]) + (r4[h, 5] + r4[h, 6]))
        place = (pl.ds(pl.multiple_of(base[h] + (z // 4) * 8, 8), 8),
                 pl.ds(pl.multiple_of(h * 512 + l * 128, 128), 128))
        out[place] = mine
        for d in zorder:
            gz[h, d] = send(out.at[place], out.at[place], s_z.at[14 + h * 7 + d - 1],
                            v_z.at[14 + h * 7 + d - 1], at_z(d))
    for copy in ez:
        copy.wait_recv()
    total = ea[2]
    for d in range(1, 8):
        total = total + er[6 + d]
    eout[...] = total

    g2 = {}
    for h in (0, 1):
        for d in (1, 7, 2, 6, 3, 5, 4):
            gz[h, d].wait_recv()
        region = out.at[pl.ds(base[h], 16), lanes[h]]
        for d in (2, 1, 3):
            g2[h, d] = send(region, region, s_mid.at[12 + h * 3 + d - 1],
                            v_mid.at[12 + h * 3 + d - 1], at_second[h](d))
    g1 = {}
    gc = {}
    for h in (0, 1):
        for d in (1, 3, 2):
            g2[h, d].wait_recv()
        region = out.at[rows_of(c, first[h]), lanes[h]]
        for d in (2, 1, 3):
            g1[h, d] = send(region, region, s_mid.at[18 + h * 3 + d - 1],
                            v_mid.at[18 + h * 3 + d - 1], at_first[h](d))
        gc[h, 0] = send(region, region, s_core.at[8 + h * 4], v_core.at[8 + h * 4], partner)
    for d in (1, 3, 2):
        for h in (0, 1):
            g1[h, d].wait_recv()
            region = out.at[rows_of(c, (first[h] + 4 - d) % 4), lanes[h]]
            gc[h, d] = send(region, region, s_core.at[8 + h * 4 + d], v_core.at[8 + h * 4 + d],
                            partner)
    for d in (0, 1, 3, 2):
        for h in (0, 1):
            gc[h, d].wait_recv()
    for copy in pending:
        copy.wait_send()


def allreduce(tot, en, collective_id=0):
    f32 = jnp.float32
    vm = pl.BlockSpec(memory_space=pltpu.VMEM)
    return pl.pallas_call(
        allreduce_kernel,
        out_shape=[jax.ShapeDtypeStruct((512, 1024), f32), jax.ShapeDtypeStruct((8, 128), f32)],
        in_specs=[vm, vm],
        out_specs=[vm, vm],
        scratch_shapes=[
            pltpu.VMEM((2, 4, 64, 512), f32),
            pltpu.VMEM((2, 4, 64, 512), f32),
            pltpu.VMEM((2, 3, 64, 512), f32),
            pltpu.VMEM((2, 64, 512), f32),
            pltpu.VMEM((2, 3, 16, 512), f32),
            pltpu.VMEM((2, 16, 512), f32),
            pltpu.VMEM((2, 7, 8, 128), f32),
            pltpu.VMEM((14, 8, 128), f32),
            pltpu.VMEM((3, 8, 128), f32),
            pltpu.SemaphoreType.DMA((16,)), pltpu.SemaphoreType.DMA((16,)),
            pltpu.SemaphoreType.DMA((24,)), pltpu.SemaphoreType.DMA((24,)),
            pltpu.SemaphoreType.DMA((28,)), pltpu.SemaphoreType.DMA((28,)),
            pltpu.SemaphoreType.DMA((14,)), pltpu.SemaphoreType.DMA((14,)),
        ],
        compiler_params=pltpu.CompilerParams(collective_id=collective_id, has_side_effects=True),
    )(tot, en)


def stencil_coefs(rows_index, total_rows):
    degrees = LAT_SOUTH + LAT_SPAN * (rows_index.astype(jnp.float32) + 0.5) / total_rows
    radians = degrees * (math.pi / 180.0)
    coriolis = 2.0 * ROTATION * jnp.sin(radians)
    north_step = EARTH_RADIUS * (LAT_SPAN / total_rows) * (math.pi / 180.0)
    east_step = EARTH_RADIUS * jnp.cos(radians) * (LON_STEP * math.pi / 180.0)
    return (-GRAVITY / (coriolis * 2.0 * north_step), GRAVITY / (coriolis * 2.0 * east_step))


DAYS, ROWS, COLS = 1024, 16, 128
CHUNKS = 4
STEP = 32


def velocity_kernel(height, land, vel, energy, hs, south, north_halo, pack, west, east_halo,
                    s_load, s_up, r_up, s_dn, r_dn, s_w, r_w, s_e, r_e):
    lon = lax.axis_index("lon")
    lat = lax.axis_index("lat")
    per = DAYS // CHUNKS
    up = ((lon + 1) % 32, lat)
    down = ((lon + 31) % 32, lat)
    right = (lon, (lat + 1) % 8)
    left = (lon, (lat + 7) % 8)

    loads = []
    for n in range(CHUNKS):
        for i in range(ROWS):
            copy = pltpu.make_async_copy(height.at[pl.ds(n * per, per), i],
                                         hs.at[i, pl.ds(n * per, per)], s_load.at[n * ROWS + i])
            copy.start()
            loads.append(copy)

    barrier = pltpu.get_barrier_semaphore()
    for dev in (up, down, right, left):
        pl.semaphore_signal(barrier, inc=1, device_id=dev, device_id_type=MESH)
    pl.semaphore_wait(barrier, 4)

    pending = []

    def send(src, dst, ssem, rsem, dev):
        copy = pltpu.make_async_remote_copy(
            src_ref=src, dst_ref=dst, send_sem=ssem, recv_sem=rsem,
            device_id=dev, device_id_type=MESH)
        copy.start()
        pending.append(copy)
        return copy

    rows = []
    for n in range(CHUNKS):
        days = pl.ds(n * per, per)
        a = send(height.at[days, ROWS - 1], south.at[days], s_up.at[n], r_up.at[n], up)
        b = send(height.at[days, 0], north_halo.at[days], s_dn.at[n], r_dn.at[n], down)
        rows.append((a, b))

    lane = lax.broadcasted_iota(jnp.int32, (1, COLS), 1)
    coef_east, coef_north = stencil_coefs(lat * COLS + lane, COLS * 8)
    ocean = land[...].astype(jnp.float32)
    ce = coef_east * ocean
    cn = coef_north * ocean
    lanes = lax.broadcasted_iota(jnp.int32, (STEP, COLS), 1)
    inner = (lane > 0) & (lane < COLS - 1)
    edge = (lanes == 0) | (lanes == COLS - 1)
    group = lanes // 4
    cb = jnp.zeros((1, COLS), jnp.float32)
    for i in range(ROWS):
        cb = jnp.where(lane // 4 == i, pltpu.roll(ce[i:i + 1], (4 * i + 2) % COLS, 1), cb)
    has_right = lat < 7
    has_left = lat > 0
    has_up = lon < 31
    has_down = lon > 0

    cols = []
    for n in range(CHUNKS):
        for i in range(ROWS):
            loads[n * ROWS + i].wait()

        def pack_step(s, _):
            at = pl.ds(pl.multiple_of(n * per + s * STEP, STEP), STEP)
            packed = jnp.zeros((STEP, COLS), jnp.float32)
            for i in range(ROWS):
                packed = jnp.where(group == i, pltpu.roll(hs[i, at], (4 * i + 2) % COLS, 1), packed)
            pack[at] = packed
            return 0

        lax.fori_loop(0, per // STEP, pack_step, 0)
        days = pl.ds(n * per, per)
        a = send(pack.at[days], west.at[days], s_w.at[n], r_w.at[n], right)
        b = send(pack.at[days], east_halo.at[days], s_e.at[n], r_e.at[n], left)
        cols.append((a, b))

    total = jnp.zeros((8, COLS), jnp.float32)
    for n in range(CHUNKS):
        for copy in rows[n] + cols[n]:
            copy.wait_recv()

        def step(s, acc):
            at = pl.ds(pl.multiple_of(n * per + s * STEP, STEP), STEP)
            mine = pack[at]
            from_right = jnp.where(has_right, east_halo[at], 0.0)
            from_left = jnp.where(has_left, west[at], 0.0)
            bound = jnp.where(
                lanes % 4 == 1,
                pltpu.roll(from_right, COLS - 1, 1) - pltpu.roll(mine, 1, 1),
                pltpu.roll(mine, COLS - 1, 1) - pltpu.roll(from_left, 1, 1)) * cb
            below = jnp.where(has_down, south[at], 0.0)
            here = hs[0, at]
            for i in range(ROWS):
                above = hs[i + 1, at] if i < ROWS - 1 else jnp.where(has_up, north_halo[at], 0.0)
                north = (above - below) * cn[i:i + 1]
                diff = pltpu.roll(here, COLS - 1, 1) - pltpu.roll(here, 1, 1)
                east = jnp.where(edge, pltpu.roll(bound, COLS - (4 * i + 2), 1), diff * ce[i:i + 1])
                vel[0, i, at] = east.astype(jnp.bfloat16)
                vel[1, i, at] = north.astype(jnp.bfloat16)
                squares = east * east + north * north
                for r in range(STEP // 8):
                    acc = acc + squares[r * 8:r * 8 + 8]
                below, here = here, above
            return acc

        total = lax.fori_loop(0, per // STEP, step, total)
    energy[...] = total
    for copy in pending:
        copy.wait_send()


def velocity(height, land_sea):
    f32 = jnp.float32
    vm = pl.BlockSpec(memory_space=pltpu.VMEM)
    dma = pltpu.SemaphoreType.DMA
    return pl.pallas_call(
        velocity_kernel,
        out_shape=[jax.ShapeDtypeStruct((2, ROWS, DAYS, COLS), jnp.bfloat16),
                   jax.ShapeDtypeStruct((8, COLS), f32)],
        in_specs=[pl.BlockSpec(memory_space=pl.ANY), vm],
        out_specs=[vm, vm],
        scratch_shapes=[pltpu.VMEM((ROWS, DAYS, COLS), f32)]
        + [pltpu.VMEM((DAYS, COLS), f32)] * 5
        + [dma((CHUNKS * ROWS,))] + [dma((CHUNKS,))] * 8,
        compiler_params=pltpu.CompilerParams(collective_id=1, has_side_effects=True),
    )(height, land_sea)


def on_device(height, land_sea, patterns):
    days, lon_cells, lat_cells = height.shape
    lat_devices = lax.axis_size("lat")
    lon_devices = lax.axis_size("lon")
    total_rows = lat_cells * lat_devices
    lat_place = lax.axis_index("lat")
    lon_place = lax.axis_index("lon")
    mode_count = patterns.shape[0]
    owned = mode_count // lat_devices
    vel, tile = velocity(height, land_sea)
    part = jnp.einsum("kcij,citj->kt", patterns, vel, preferred_element_type=jnp.float32)
    totals, energies = allreduce(part, tile)
    energy = jnp.sum(energies)
    cell_total = 2.0 * days * lon_cells * lon_devices * total_rows
    centered = totals - jnp.mean(totals, axis=1, keepdims=True)
    normed = centered / jnp.sqrt(energy / cell_total + 1e-06)
    my_rows = lax.dynamic_slice_in_dim(normed, lat_place * owned, owned, 0)
    padded_rows = jnp.concatenate([my_rows, jnp.zeros_like(my_rows)], axis=1)
    lag = lon_place * LAG_DEV + 0
    shifted = lax.dynamic_slice_in_dim(padded_rows, lag, days, 1)
    product = lax.dot_general(
        shifted,
        normed,
        (((1,), (1,)), ((), ())),
        precision=lax.Precision.HIGHEST,
        preferred_element_type=jnp.float32,
    )
    results = [product / (days - lag).astype(jnp.float32)]
    return jnp.stack(results, axis=0)


def solution(mesh):
    placed = (P(None, "lon", "lat"), P("lon", "lat"), P(None, None, "lon", "lat"))
    return jax.shard_map(
        on_device, mesh=mesh, in_specs=placed, out_specs=P("lon", "lat", None), check_vma=False
    )
```
